256 devices in a mesh: batch: 64 (over x, z, core), proto: 4 (over y).
Axes of the slice: x: 4, y: 4, z: 8, core: 2. Of those that a mesh axis runs over, the one named last changes fastest.
Arguments:
- embeddings: bfloat16 [16384, 256], P('batch'), may hold values from -64 to 64
- prototypes: bfloat16 [65536, 256], P('proto'), may hold values from -1 to 1
- row_cot: float32 [16384], P('batch'), may hold values from -6 to 6
- col_cot: float32 [65536], P('proto'), may hold values from -6 to 6
Outputs:
- embed_grad: float32 [16384, 256], P('batch')
- proto_grad: float32 [65536, 256], P(('proto', 'batch'))
The draws below stay inside these ranges and needn't reach their ends.
All inputs are finite; a program needn't handle non-finite values.
Results may differ from the reference program's by a relative error of at most 0.0033.
Values may be sent and summed in bfloat16 or wider, within the bound.
A program may use at most 128 MiB of HBM per device.

```python
import math
import jax
import jax.numpy as jnp
from jax import lax

D = 256
B_DEV = 256
K = 65536
B = 16384


def draw_both(key):
    key_proto = jax.random.fold_in(key, 11)
    key_embed = jax.random.fold_in(key, 12)
    protos = jnp.clip(jax.random.normal(key_proto, (K, D), jnp.float32) / math.sqrt(D), -1.0, 1.0)
    embeds = jnp.clip(jax.random.normal(key_embed, (B, D), jnp.float32), -6.0, 6.0)
    return (embeds, protos)


def draw_embeddings(key, part):
    return draw_both(key)[0].astype(jnp.bfloat16)


def draw_prototypes(key, part):
    return draw_both(key)[1].astype(jnp.bfloat16)


def shard_levels(key, dims, shards, low, top_value):
    def one(position, shards_of):
        heights = jax.random.uniform(jax.random.fold_in(jax.random.fold_in(key, 6), position), (shards_of,), jnp.float32, low / len(shards), top_value / len(shards))
        return jnp.repeat(jnp.exp(heights), dims[position] // shards_of).reshape((-1,) + (1,) * (len(dims) - position - 1))

    factor_of = one(*shards[0])
    for cut in shards[1:]:
        factor_of = factor_of * one(*cut)
    return factor_of


def normal_values(stream_key, extent, spread, reach, cuts=(), kind=jnp.bfloat16):
    level = shard_levels(stream_key, extent, cuts, -0.22, 0.18) if cuts else 1.0
    drawn = jax.random.normal(stream_key, extent, jnp.float32) * spread * level
    return jnp.minimum(jnp.maximum(drawn, -reach), reach).astype(kind)


def setup_inputs(seed: int = 0) -> dict:
    streams_of = jax.random.split(jax.random.key(seed), 5)
    embeddings = draw_embeddings(jax.random.fold_in(streams_of[4], 71), 0)
    prototypes = draw_prototypes(jax.random.fold_in(streams_of[4], 71), 0)
    row_cot = normal_values(streams_of[2], (B,), 1.0, 6.0, ((0, 64),), jnp.float32)
    col_cot = normal_values(streams_of[3], (K,), 1.0, 6.0, ((0, 4),), jnp.float32)
    return dict(embeddings=embeddings, prototypes=prototypes, row_cot=row_cot, col_cot=col_cot)


score_scale = 4.0


def block_scores(block_rows, prototypes):
    return jnp.dot(block_rows, prototypes.T, preferred_element_type=jnp.float32) * score_scale


def reference(embeddings, prototypes, row_cot, col_cot):
    log_rows = math.log(B)
    log_cols = math.log(K)
    blocks = B // B_DEV
    row_blocks = embeddings.reshape(blocks, B_DEV, D)

    def split(vector):
        return vector.reshape(blocks, B_DEV)

    def row_lse(col_pot):
        def one(block_rows):
            shifted = block_scores(block_rows, prototypes) + col_pot[None, :]
            peak = jnp.max(shifted, axis=1)
            return peak + jnp.log(jnp.sum(jnp.exp(shifted - peak[:, None]), axis=1))
        return lax.map(one, row_blocks).reshape(B)

    def col_lse(row_pot):
        def step(carry, items):
            block_rows, pot_block = items
            shifted = block_scores(block_rows, prototypes) + pot_block[:, None]
            top = jnp.maximum(carry[0], jnp.max(shifted, axis=0))
            mass = carry[1] * jnp.exp(carry[0] - top) + jnp.sum(jnp.exp(shifted - top[None, :]), axis=0)
            return (top, mass), None
        init = (jnp.full((K,), -jnp.inf, jnp.float32), jnp.zeros((K,), jnp.float32))
        (top, mass), _ = lax.scan(step, init, (row_blocks, split(row_pot)))
        return top + jnp.log(mass)

    f_one = -log_rows - row_lse(jnp.zeros((K,), jnp.float32))
    g_one = -log_cols - col_lse(f_one)
    f_two = -log_rows - row_lse(g_one)
    g_two = -log_cols - col_lse(f_two)

    def first_adj(items):
        block_rows, ftwo_block = items
        plan_four = jnp.exp(block_scores(block_rows, prototypes) + ftwo_block[:, None] + g_two[None, :] + log_cols)
        return jnp.sum(plan_four * col_cot[None, :], axis=1)
    bar_ftwo = row_cot - lax.map(first_adj, (row_blocks, split(f_two))).reshape(B)

    def second_adj(carry, items):
        block_rows, ftwo_block, bar_block = items
        plan_three = jnp.exp(block_scores(block_rows, prototypes) + ftwo_block[:, None] + g_one[None, :] + log_rows)
        return carry + jnp.sum(bar_block[:, None] * plan_three, axis=0), None
    col_total, _ = lax.scan(second_adj, jnp.zeros((K,), jnp.float32), (row_blocks, split(f_two), split(bar_ftwo)))
    bar_gone = -col_total

    def third_adj(items):
        block_rows, fone_block = items
        plan_two = jnp.exp(block_scores(block_rows, prototypes) + fone_block[:, None] + g_one[None, :] + log_cols)
        return jnp.sum(plan_two * bar_gone[None, :], axis=1)
    bar_fone = -lax.map(third_adj, (row_blocks, split(f_one))).reshape(B)

    def grads(carry, items):
        block_rows, fone_block, ftwo_block, bar_two_block, bar_one_block = items
        scores = block_scores(block_rows, prototypes)
        plan_one = jnp.exp(scores + fone_block[:, None] + log_rows)
        plan_two = jnp.exp(scores + fone_block[:, None] + g_one[None, :] + log_cols)
        plan_three = jnp.exp(scores + ftwo_block[:, None] + g_one[None, :] + log_rows)
        plan_four = jnp.exp(scores + ftwo_block[:, None] + g_two[None, :] + log_cols)
        adjoint = -(col_cot[None, :] * plan_four + bar_two_block[:, None] * plan_three
                    + bar_gone[None, :] * plan_two + bar_one_block[:, None] * plan_one)
        adjoint = adjoint.astype(jnp.bfloat16)
        row_grad = jnp.dot(adjoint, prototypes, preferred_element_type=jnp.float32) * score_scale
        col_part = lax.dot_general(adjoint, block_rows, (((0,), (0,)), ((), ())), preferred_element_type=jnp.float32)
        return carry + col_part * score_scale, row_grad

    proto_grad, embed_blocks = lax.scan(grads, jnp.zeros((K, D), jnp.float32),
                                        (row_blocks, split(f_one), split(f_two), split(bar_ftwo), split(bar_fone)))
    return embed_blocks.reshape(B, D), proto_grad
```

```python
import math

import jax
import jax.numpy as jnp
from jax import lax
from jax.experimental import pallas as pl
from jax.experimental.pallas import tpu as pltpu
from jax.sharding import Mesh
from jax.sharding import PartitionSpec as P

MESH = pl.DeviceIdType.MESH
LOG2E = math.log2(math.e)
SCALE = 4.0
SCALE2 = SCALE * LOG2E
F32 = jnp.float32
BF16 = jnp.bfloat16
NX, NZ, NC, NY = 4, 8, 2, 4
ROWS, COLS, D = 256, 16384, 256
TILES = COLS // 128
LOG2_B = math.log2(ROWS * NX * NZ * NC)
N_B = float(ROWS * NX * NZ * NC)
N_K = float(COLS * NY)


def dot_nt(a, b):
    return lax.dot_general(a, b, (((1,), (1,)), ((), ())), preferred_element_type=F32)


def lse2(parts):
    top = parts[0]
    for p in parts[1:]:
        top = jnp.maximum(top, p)
    mass = jnp.exp2(parts[0] - top)
    for p in parts[1:]:
        mass = mass + jnp.exp2(p - top)
    return top + jnp.log(mass) * LOG2E


def total(parts):
    out = parts[0]
    for p in parts[1:]:
        out = out + p
    return out


def row_form(acc):
    return jnp.sum(acc.T, axis=0, keepdims=True)


def spread(row):
    return jnp.broadcast_to(row, (128, row.shape[1])).T


def kernel(emb_hbm, protos_hbm, rcot_ref, ccot_ref, eg_ref, pg_ref,
           S, PV, EA, MX, FB, UB, XB, CM, CS, W, A, H, LG, V, ADJ, RP, PG, PR, LB, AB, CB, DB, ADJ2,
           rbuf, cloc, c1, c2, c3, G, Y, EB, EO,
           psem, esem, rs, rr, s1, r1, s2, r2, s3, r3, es_z, es_x, er, gs, gr, ys, yr, eb_s, eb_r, eo_s, eo_r, pr_s, pr_r):
    x, z, c, y = lax.axis_index("x"), lax.axis_index("z"), lax.axis_index("c"), lax.axis_index("p")
    k = x * NC + c
    sent = []

    def send(src, dst, ssem, rsem, where):
        copy = pltpu.make_async_remote_copy(src_ref=src, dst_ref=dst, send_sem=ssem, recv_sem=rsem,
                                            device_id=where, device_id_type=MESH)
        copy.start()
        sent.append(copy)

    def landed(ref, ssem, rsem, where):
        pltpu.make_async_remote_copy(src_ref=ref, dst_ref=ref, send_sem=ssem, recv_sem=rsem,
                                     device_id=where, device_id_type=MESH).wait_recv()

    def at_y(d):
        return (y + d) % NY

    def at_z(d):
        return (z + d) % NZ

    def at_x(d):
        return (x + d) % NX

    def at_k(d):
        return (k + d) % (NX * NC)

    def xc(kk):
        return {"x": kk // NC, "c": kk % NC}

    barrier = pltpu.get_barrier_semaphore()
    for d in range(1, NY):
        pl.semaphore_signal(barrier, inc=1, device_id={"p": at_y(d)}, device_id_type=MESH)
    for d in range(1, NX * NC):
        pl.semaphore_signal(barrier, inc=1, device_id=xc(at_k(d)), device_id_type=MESH)
    for d in range(1, NZ):
        pl.semaphore_signal(barrier, inc=1, device_id={"z": at_z(d)}, device_id_type=MESH)

    own = pltpu.make_async_copy(emb_hbm, EA.at[x, z], esem)
    own.start()
    step = COLS // 8
    loads = [pltpu.make_async_copy(protos_hbm.at[pl.ds(q * step, step)], PV.at[pl.ds(q * step, step)], psem.at[q])
             for q in range(8)]
    for q in loads:
        q.start()
    MX[...] = jnp.full((ROWS, 128), -jnp.inf, F32)
    own.wait()

    def score_chunk(q, _):
        at = pl.multiple_of(q * 512, 512)
        s = dot_nt(EA[x, z], PV[pl.ds(at, 512), :]) * SCALE2
        m = MX[...]
        for j in range(4):
            t = s[:, j * 128:(j + 1) * 128]
            S[4 * q + j] = t
            m = jnp.maximum(m, t)
        MX[...] = m
        return 0

    def x_stage(r):
        zb = at_z(r)
        if r:
            landed(EA.at[x, zb], es_z.at[r], er.at[x, zb], {"z": zb})
        for d in range(1, NX):
            send(EA.at[x, zb], EA.at[x, zb], es_x.at[r, d], er.at[x, zb], {"x": at_x(d)})

    def z_stage(d):
        send(EA.at[x, z], EA.at[x, z], es_z.at[NZ - d], er.at[x, z], {"z": at_z(d)})

    for q in range(8):
        loads[q].wait()
        lax.fori_loop(q * 4, q * 4 + 4, score_chunk, 0)
        if q == 3:
            pl.semaphore_wait(barrier, NY - 1 + NX * NC - 1 + NZ - 1)
            for d in (1, 7, 2, 6):
                z_stage(d)
            x_stage(0)

    def mass_tile(t, acc):
        for j in range(2):
            acc = acc + jnp.exp2(S[2 * t + j] - MX[...])
        return acc

    mass = lax.fori_loop(0, TILES // 2, mass_tile, jnp.zeros((ROWS, 128), F32))
    mt = MX[...].T
    top = jnp.max(mt, axis=0, keepdims=True)
    loc = top + jnp.log(jnp.sum(mass.T * jnp.exp2(mt - top), axis=0, keepdims=True)) * LOG2E

    def row_all(i, row, combine):
        rbuf[i, y] = row
        for d in range(1, NY):
            send(rbuf.at[i, y], rbuf.at[i, y], rs.at[i, d], rr.at[i, y], {"p": at_y(d)})
        for d in range(1, NY):
            f = at_y(d)
            landed(rbuf.at[i, f], rs.at[i, d], rr.at[i, f], {"p": f})
        return combine([rbuf[i, j] for j in range(NY)])

    def col_all(i, col, combine, between):
        cloc[i] = col.reshape(8, TILES // 8, 128)
        for d in range(1, 8):
            f = at_k(d)
            send(cloc.at[i, f], c1.at[i, k], s1.at[i, d], r1.at[i, k], xc(f))
        c1[i, k] = cloc[i, k]
        for d in range(1, 8):
            f = at_k(d)
            landed(c1.at[i, f], s1.at[i, d], r1.at[i, f], xc(f))
        c2[i, z] = combine([c1[i, j] for j in range(8)])
        for d in range(1, NZ):
            send(c2.at[i, z], c2.at[i, z], s2.at[i, d], r2.at[i, z], {"z": at_z(d)})
        between()
        for d in range(1, NZ):
            f = at_z(d)
            landed(c2.at[i, f], s2.at[i, d], r2.at[i, f], {"z": f})
        c3[i, k] = combine([c2[i, j] for j in range(NZ)])
        for d in range(1, 8):
            send(c3.at[i, k], c3.at[i, k], s3.at[i, d], r3.at[i, k], xc(at_k(d)))
        for d in range(1, 8):
            f = at_k(d)
            landed(c3.at[i, f], s3.at[i, d], r3.at[i, f], xc(f))
        return c3[i].reshape(TILES, 128)

    def row_pass():
        def tile(t, acc):
            for j in range(4):
                acc = acc + S[4 * t + j] * W[pl.ds(4 * t + j, 1), :]
            return acc
        return row_form(lax.fori_loop(0, TILES // 4, tile, jnp.zeros((ROWS, 128), F32)))

    def col_pass(weights):
        def tile(t, _):
            for j in range(2):
                CS[pl.ds(2 * t + j, 1), :] = jnp.sum(S[2 * t + j] * weights[...], axis=0, keepdims=True)
            return 0
        lax.fori_loop(0, TILES // 2, tile, 0)
        return CS[...]

    f_one = -LOG2_B - row_all(0, loc, lse2)
    FB[...] = spread(f_one)

    def plan_tile(t, _):
        v = S[t] + FB[...]
        m = jnp.max(v, axis=0, keepdims=True)
        e = jnp.exp2(v - m)
        S[t] = e
        CM[pl.ds(t, 1), :] = m
        CS[pl.ds(t, 1), :] = jnp.sum(e, axis=0, keepdims=True)
        return 0

    lax.fori_loop(0, TILES, plan_tile, 0)
    big = col_all(0, CM[...] + jnp.log(CS[...]) * LOG2E, lse2, lambda: x_stage(1))
    LG[...] = big
    H[...] = jnp.exp2(CM[...] - big)
    for d in (3, 5):
        z_stage(d)
    x_stage(7)
    W[...] = H[...]
    u = (N_K / N_B) / row_all(1, row_pass(), total)
    UB[...] = spread(u)
    v = 1.0 / col_all(1, H[...] * col_pass(UB), total, lambda: x_stage(2))
    V[...] = -(v * ccot_ref[...])
    z_stage(4)
    x_stage(6)
    A[...] = H[...] * V[...]
    W[...] = A[...]
    bar_two = rcot_ref[...] + u * row_all(2, row_pass(), total)
    xr = bar_two * u
    XB[...] = spread(xr)
    xn = xr * -(N_B / N_K)
    for j, vec in enumerate((f_one, u, xn)):
        G[x, z, 2 * j:2 * j + 1] = vec[:, :128]
        G[x, z, 2 * j + 1:2 * j + 2] = vec[:, 128:]
    G[x, z, 6:8] = jnp.zeros((2, 128), F32)
    for d in range(1, NZ):
        send(G.at[x, z], G.at[x, z], gs.at[0, d], gr.at[x, z], {"z": at_z(d)})
    neg_bar_one = (N_B / N_K) * col_all(2, H[...] * col_pass(XB), total, lambda: x_stage(3))
    for d in range(1, NZ):
        f = at_z(d)
        landed(G.at[x, f], gs.at[0, d], gr.at[x, f], {"z": f})
    for d in range(1, NX):
        send(G.at[x], G.at[x], gs.at[1, d], yr.at[0, x], {"x": at_x(d)})
    x_stage(5)
    x_stage(4)
    CS[...] = neg_bar_one
    W[...] = H[...] * neg_bar_one
    yn = -row_all(3, row_pass(), total)
    Y[x, z, 0:1] = yn[:, :128]
    Y[x, z, 1:2] = yn[:, 128:]
    for d in range(1, NZ):
        send(Y.at[x, z], Y.at[x, z], ys.at[0, d], gr.at[NX + x, z], {"z": at_z(d)})
    XB[...] = XB[...] * -(N_B / N_K)
    FB[...] = spread(yn)
    CM[...] = jnp.exp2(CM[...]) * N_B
    RP[...] = jnp.zeros((ROWS, D), F32)

    def grad_chunk(q, _):
        at = pl.multiple_of(q * 512, 512)
        for j in range(4):
            t = 4 * q + j
            g = UB[...] * A[pl.ds(t, 1), :] + XB[...] * H[pl.ds(t, 1), :]
            g = g + FB[...] * CM[pl.ds(t, 1), :] + W[pl.ds(t, 1), :]
            ADJ[:, j * 128:(j + 1) * 128] = (S[t] * g).astype(BF16)
        RP[...] += jnp.dot(ADJ[...], PV[pl.ds(at, 512), :], preferred_element_type=F32)
        return 0

    half = COLS // 1024
    lax.fori_loop(0, half, grad_chunk, 0)
    for d in range(1, NZ):
        f = at_z(d)
        landed(Y.at[x, f], ys.at[0, d], gr.at[NX + x, f], {"z": f})
    for d in range(1, NX):
        send(Y.at[x], Y.at[x], ys.at[1, d], yr.at[1, x], {"x": at_x(d)})
    lax.fori_loop(half, 2 * half, grad_chunk, 0)
    piece = ROWS // NY

    def quarter(j):
        return RP.at[pl.ds(pl.multiple_of(j * piece, piece), piece)]

    for d in range(1, NY):
        f = at_y(d)
        send(quarter(f), EB.at[y], eb_s.at[d], eb_r.at[y], {"p": f})
    EB[y] = quarter(y)[...]

    chip = x * NZ + z
    pown = PV.at[pl.ds(pl.multiple_of(chip * 512, 512), 512)]
    for j in range(4):
        at = pl.ds(j * 128, 128)
        line = pl.ds(chip * 4 + j, 1)
        LB[at, :] = spread(LG[line, :])
        AB[at, :] = spread(V[line, :])
        CB[at, :] = spread(CS[line, :])
        DB[at, :] = spread(jnp.exp2(LG[line, :]) * N_B)
    PG[...] = jnp.zeros((2 * ROWS, D), F32)
    for d in range(1, NX):
        f = at_x(d)
        landed(G.at[f], gs.at[1, d], yr.at[0, f], {"x": f})
        landed(Y.at[f], ys.at[1, d], yr.at[1, f], {"x": f})
        for r in range(NZ):
            zb = at_z(r)
            landed(EA.at[f, zb], es_x.at[r, d], er.at[f, zb], {"x": f})

    def back_block(o, _):
        xb, zb = o // NZ, o % NZ
        s = dot_nt(pown[...], EA[xb, zb]) * SCALE2
        for j in range(4):
            at = slice(j * 128, (j + 1) * 128)
            for n in range(2):
                e = jnp.exp2(s[at, n * 128:(n + 1) * 128] + G[xb, zb, n:n + 1] - LB[at, :])
                g = AB[at, :] * G[xb, zb, 2 + n:3 + n] + G[xb, zb, 4 + n:5 + n]
                g = g + CB[at, :] + DB[at, :] * Y[xb, zb, n:n + 1]
                ADJ2[at, n * 128:(n + 1) * 128] = (e * g).astype(BF16)
        PG[...] += jnp.dot(ADJ2[...], EA[xb, zb], preferred_element_type=F32)
        return 0

    mid = NX * NZ // 2
    lax.fori_loop(0, mid, back_block, 0)
    for d in range(1, NY):
        f = at_y(d)
        landed(EB.at[f], eb_s.at[d], eb_r.at[f], {"p": f})
    EO[y] = total([EB[j] for j in range(NY)]) * SCALE
    for d in range(1, NY):
        send(EO.at[y], EO.at[y], eo_s.at[d], eo_r.at[y], {"p": at_y(d)})
    lax.fori_loop(mid, 2 * mid, back_block, 0)
    there = PG.at[pl.ds(pl.multiple_of((1 - c) * ROWS, ROWS), ROWS)]
    send(there, PR, pr_s, pr_r, {"c": 1 - c})
    for d in range(1, NY):
        f = at_y(d)
        landed(EO.at[f], eo_s.at[d], eo_r.at[f], {"p": f})
    eg_ref[...] = EO[...].reshape(ROWS, D)
    landed(PR, pr_s, pr_r, {"c": 1 - c})
    pg_ref[...] = (PG[pl.ds(pl.multiple_of(c * ROWS, ROWS), ROWS), :] + PR[...]) * SCALE
    for copy in sent:
        copy.wait_send()


def step(embeddings, prototypes, row_cot, col_cot):
    vm = pltpu.VMEM
    dma = pltpu.SemaphoreType.DMA
    wide = vm((ROWS, 128), F32)
    line = vm((TILES, 128), F32)
    scratch = [
        vm((TILES, ROWS, 128), F32), vm((COLS, D), BF16), vm((NX, NZ, ROWS, D), BF16),
        wide, wide, wide, wide,
        line, line, line, line, line, line, line,
        vm((ROWS, 512), BF16), vm((ROWS, D), F32), vm((2 * ROWS, D), F32), vm((ROWS, D), F32),
        vm((512, 128), F32), vm((512, 128), F32), vm((512, 128), F32), vm((512, 128), F32), vm((512, ROWS), BF16),
        vm((4, NY, 1, ROWS), F32), vm((3, 8, TILES // 8, 128), F32), vm((3, 8, TILES // 8, 128), F32),
        vm((3, NZ, TILES // 8, 128), F32), vm((3, 8, TILES // 8, 128), F32),
        vm((NX, NZ, 8, 128), F32), vm((NX, NZ, 2, 128), F32),
        vm((NY, ROWS // NY, D), F32), vm((NY, ROWS // NY, D), F32),
        dma((8,)), dma(()), dma((4, NY)), dma((4, NY)),
        dma((3, 8)), dma((3, 8)), dma((3, 8)), dma((3, 8)), dma((3, 8)), dma((3, 8)),
        dma((NZ,)), dma((NZ, NX)), dma((NX, NZ)), dma((2, NZ)), dma((2 * NX, NZ)),
        dma((2, NZ)), dma((2, NX)),
        dma((NY,)), dma((NY,)), dma((NY,)), dma((NY,)), dma(()), dma(()),
    ]
    anywhere = pl.BlockSpec(memory_space=pl.ANY)
    inside = pl.BlockSpec(memory_space=pltpu.VMEM)
    return pl.pallas_call(
        kernel,
        out_shape=(jax.ShapeDtypeStruct((ROWS, D), F32), jax.ShapeDtypeStruct((ROWS, D), F32)),
        in_specs=[anywhere, anywhere, inside, inside],
        out_specs=(inside, inside),
        scratch_shapes=scratch,
        compiler_params=pltpu.CompilerParams(collective_id=0, has_side_effects=True, vmem_limit_bytes=60 << 20),
        name="sinkhorn_back",
    )(embeddings, prototypes, row_cot.reshape(1, ROWS), col_cot.reshape(TILES, 128))


def solution(mesh):
    split = Mesh(mesh.devices.reshape(NX, NZ, NC, NY), ("x", "z", "c", "p"))
    rows = ("x", "z", "c")
    return jax.shard_map(
        step,
        mesh=split,
        in_specs=(P(rows, None), P("p", None), P(rows), P("p")),
        out_specs=(P(rows, None), P(("p",) + rows, None)),
        check_vma=False,
    )
```

```python
import math

import jax
import jax.numpy as jnp
from jax import lax
from jax.experimental import pallas as pl
from jax.experimental.pallas import tpu as pltpu
from jax.sharding import Mesh
from jax.sharding import PartitionSpec as P

MESH = pl.DeviceIdType.MESH
LOG2E = math.log2(math.e)
SCALE = 4.0
SCALE2 = SCALE * LOG2E
F32 = jnp.float32
BF16 = jnp.bfloat16
NX, NZ, NC, NY = 4, 8, 2, 4
ROWS, COLS, D = 256, 16384, 256
TILES = COLS // 128
LOG2_B = math.log2(ROWS * NX * NZ * NC)
N_B = float(ROWS * NX * NZ * NC)
N_K = float(COLS * NY)


def dot_nt(a, b):
    return lax.dot_general(a, b, (((1,), (1,)), ((), ())), preferred_element_type=F32)


def lse2(parts):
    top = parts[0]
    for p in parts[1:]:
        top = jnp.maximum(top, p)
    mass = jnp.exp2(parts[0] - top)
    for p in parts[1:]:
        mass = mass + jnp.exp2(p - top)
    return top + jnp.log(mass) * LOG2E


def total(parts):
    out = parts[0]
    for p in parts[1:]:
        out = out + p
    return out


def row_form(acc):
    return jnp.sum(acc.T, axis=0, keepdims=True)


def spread(row):
    return jnp.broadcast_to(row, (128, row.shape[1])).T


def kernel(emb_hbm, protos_hbm, rcot_ref, ccot_ref, eg_ref, pg_ref,
           S, PV, EA, MX, FB, UB, XB, CM, CS, W, A, H, LG, V, ADJ, RP, PG, PR, LB, AB, CB, DB, ADJ2, ST, T,
           rbuf, cloc, c1, c2, c3, G, Y, EB, EO,
           psem, esem, rs, rr, s1, r1, s2, r2, s3, r3, es_z, es_x, er, gs, gr, ys, yr, eb_s, eb_r, eo_s, eo_r, pr_s, pr_r):
    x, z, c, y = lax.axis_index("x"), lax.axis_index("z"), lax.axis_index("c"), lax.axis_index("p")
    k = x * NC + c
    sent = []

    def send(src, dst, ssem, rsem, where):
        copy = pltpu.make_async_remote_copy(src_ref=src, dst_ref=dst, send_sem=ssem, recv_sem=rsem,
                                            device_id=where, device_id_type=MESH)
        copy.start()
        sent.append(copy)

    def landed(ref, ssem, rsem, where):
        pltpu.make_async_remote_copy(src_ref=ref, dst_ref=ref, send_sem=ssem, recv_sem=rsem,
                                     device_id=where, device_id_type=MESH).wait_recv()

    def at_y(d):
        return (y + d) % NY

    def at_z(d):
        return (z + d) % NZ

    def at_x(d):
        return (x + d) % NX

    def at_k(d):
        return (k + d) % (NX * NC)

    def xc(kk):
        return {"x": kk // NC, "c": kk % NC}

    barrier = pltpu.get_barrier_semaphore()
    for d in range(1, NY):
        pl.semaphore_signal(barrier, inc=1, device_id={"p": at_y(d)}, device_id_type=MESH)
    for d in range(1, NX * NC):
        pl.semaphore_signal(barrier, inc=1, device_id=xc(at_k(d)), device_id_type=MESH)
    for d in range(1, NZ):
        pl.semaphore_signal(barrier, inc=1, device_id={"z": at_z(d)}, device_id_type=MESH)

    own = pltpu.make_async_copy(emb_hbm, EA.at[x, z], esem)
    own.start()
    step = COLS // 8
    loads = [pltpu.make_async_copy(protos_hbm.at[pl.ds(q * step, step)], PV.at[pl.ds(q * step, step)], psem.at[q])
             for q in range(8)]
    for q in loads:
        q.start()
    MX[...] = jnp.full((ROWS, 128), -jnp.inf, F32)
    own.wait()

    def fold(q, n):
        for b in range(4):
            at = slice(b * 64, (b + 1) * 64)
            tiles = [T[n, at, j * 128:(j + 1) * 128] for j in range(4)]
            old = MX[at, :]
            new = jnp.maximum(jnp.maximum(jnp.maximum(tiles[0], tiles[1]), jnp.maximum(tiles[2], tiles[3])), old)
            mass = XB[at, :] * jnp.exp2(old - new)
            more = (jnp.exp2(tiles[0] - new) + jnp.exp2(tiles[1] - new)) + (jnp.exp2(tiles[2] - new) + jnp.exp2(tiles[3] - new))
            XB[at, :] = mass + more
            MX[at, :] = new
            for j in range(4):
                S[4 * q + j, at, :] = tiles[j]

    def score(q, n):
        at = pl.multiple_of(q * 512, 512)
        T[n] = dot_nt(EA[x, z], PV[pl.ds(at, 512), :]) * SCALE2

    def score_chunk(q, _):
        score(2 * q + 1, 1)
        fold(2 * q, 0)
        score(jnp.minimum(2 * q + 2, TILES // 4 - 1), 0)
        fold(2 * q + 1, 1)
        return 0

    def x_stage(r):
        zb = at_z(r)
        if r:
            landed(EA.at[x, zb], es_z.at[r], er.at[x, zb], {"z": zb})
        for d in range(1, NX):
            send(EA.at[x, zb], EA.at[x, zb], es_x.at[r, d], er.at[x, zb], {"x": at_x(d)})

    def z_stage(d):
        send(EA.at[x, z], EA.at[x, z], es_z.at[NZ - d], er.at[x, z], {"z": at_z(d)})

    XB[...] = jnp.zeros((ROWS, 128), F32)
    loads[0].wait()
    score(0, 0)

    def part(q, _):
        pltpu.make_async_copy(protos_hbm.at[pl.ds(q * step, step)], PV.at[pl.ds(q * step, step)], psem.at[q]).wait()
        lax.fori_loop(q * 2 - 2, q * 2, score_chunk, 0)
        return 0

    lax.fori_loop(1, 4, part, 0)
    pl.semaphore_wait(barrier, NY - 1 + NX * NC - 1 + NZ - 1)
    for d in (1, 7, 2, 6):
        z_stage(d)
    x_stage(0)
    lax.fori_loop(4, 8, part, 0)
    lax.fori_loop(14, 16, score_chunk, 0)
    mt = MX[...].T
    top = jnp.max(mt, axis=0, keepdims=True)
    loc = top + jnp.log(jnp.sum(XB[...].T * jnp.exp2(mt - top), axis=0, keepdims=True)) * LOG2E

    def row_all(i, row, combine):
        rbuf[i, y] = row
        for d in range(1, NY):
            send(rbuf.at[i, y], rbuf.at[i, y], rs.at[i, d], rr.at[i, y], {"p": at_y(d)})
        for d in range(1, NY):
            f = at_y(d)
            landed(rbuf.at[i, f], rs.at[i, d], rr.at[i, f], {"p": f})
        return combine([rbuf[i, j] for j in range(NY)])

    def col_all(i, col, combine, between):
        cloc[i] = col.reshape(8, TILES // 8, 128)
        for d in range(1, 8):
            f = at_k(d)
            send(cloc.at[i, f], c1.at[i, k], s1.at[i, d], r1.at[i, k], xc(f))
        c1[i, k] = cloc[i, k]
        for d in range(1, 8):
            f = at_k(d)
            landed(c1.at[i, f], s1.at[i, d], r1.at[i, f], xc(f))
        c2[i, z] = combine([c1[i, j] for j in range(8)])
        for d in range(1, NZ):
            send(c2.at[i, z], c2.at[i, z], s2.at[i, d], r2.at[i, z], {"z": at_z(d)})
        between()
        for d in range(1, NZ):
            f = at_z(d)
            landed(c2.at[i, f], s2.at[i, d], r2.at[i, f], {"z": f})
        c3[i, k] = combine([c2[i, j] for j in range(NZ)])
        for d in range(1, 8):
            send(c3.at[i, k], c3.at[i, k], s3.at[i, d], r3.at[i, k], xc(at_k(d)))
        for d in range(1, 8):
            f = at_k(d)
            landed(c3.at[i, f], s3.at[i, d], r3.at[i, f], xc(f))
        return c3[i].reshape(TILES, 128)

    def row_pass():
        for b in range(4):
            at = slice(b * 64, (b + 1) * 64)

            def tile(t, acc):
                even, odd = acc
                for j in range(0, 8, 2):
                    even = even + S[8 * t + j, at, :] * W[pl.ds(8 * t + j, 1), :]
                    odd = odd + S[8 * t + j + 1, at, :] * W[pl.ds(8 * t + j + 1, 1), :]
                return even, odd

            none = jnp.zeros((64, 128), F32)
            even, odd = lax.fori_loop(0, TILES // 8, tile, (none, none))
            MX[at, :] = even + odd
        return row_form(MX[...])

    def col_pass(weights):
        def tile(t, _):
            acc = [None] * 4
            for b in range(4):
                at = slice(b * 64, (b + 1) * 64)
                w = weights[at, :]
                for j in range(4):
                    term = S[4 * t + j, at, :] * w
                    acc[j] = term if b == 0 else acc[j] + term
            for j in range(4):
                CS[pl.ds(4 * t + j, 1), :] = jnp.sum(acc[j], axis=0, keepdims=True)
            return 0
        lax.fori_loop(0, TILES // 4, tile, 0)
        return CS[...]

    f_one = -LOG2_B - row_all(0, loc, lse2)
    FB[...] = spread(f_one)

    def tops(t):
        best = [None, None]
        for b in range(4):
            at = slice(b * 64, (b + 1) * 64)
            f = FB[at, :]
            for j in range(2):
                here = S[t + j, at, :] + f
                best[j] = here if b == 0 else jnp.maximum(best[j], here)
        return tuple(jnp.max(m, axis=0, keepdims=True) for m in best)

    def plan_tile(t, m):
        later = tops(jnp.minimum(2 * t + 2, TILES - 2))
        acc = [None, None]
        for b in range(4):
            at = slice(b * 64, (b + 1) * 64)
            f = FB[at, :]
            for j in range(2):
                e = jnp.exp2(S[2 * t + j, at, :] + f - m[j])
                S[2 * t + j, at, :] = e
                acc[j] = e if b == 0 else acc[j] + e
        for j in range(2):
            CM[pl.ds(2 * t + j, 1), :] = m[j]
            CS[pl.ds(2 * t + j, 1), :] = jnp.sum(acc[j], axis=0, keepdims=True)
        return later

    lax.fori_loop(0, TILES // 2, plan_tile, tops(0))
    big = col_all(0, CM[...] + jnp.log(CS[...]) * LOG2E, lse2, lambda: x_stage(1))
    LG[...] = big
    H[...] = jnp.exp2(CM[...] - big)
    for d in (3, 5):
        z_stage(d)
    x_stage(7)
    W[...] = H[...]
    u = (N_K / N_B) / row_all(1, row_pass(), total)
    UB[...] = spread(u)
    v = 1.0 / col_all(1, H[...] * col_pass(UB), total, lambda: x_stage(2))
    V[...] = -(v * ccot_ref[...])
    z_stage(4)
    x_stage(6)
    A[...] = H[...] * V[...]
    W[...] = A[...]
    bar_two = rcot_ref[...] + u * row_all(2, row_pass(), total)
    xr = bar_two * u
    XB[...] = spread(xr)
    xn = xr * -(N_B / N_K)
    for j, vec in enumerate((f_one, u, xn)):
        G[x, z, 2 * j:2 * j + 1] = vec[:, :128]
        G[x, z, 2 * j + 1:2 * j + 2] = vec[:, 128:]
    G[x, z, 6:8] = jnp.zeros((2, 128), F32)
    for d in range(1, NZ):
        send(G.at[x, z], G.at[x, z], gs.at[0, d], gr.at[x, z], {"z": at_z(d)})
    neg_bar_one = (N_B / N_K) * col_all(2, H[...] * col_pass(XB), total, lambda: x_stage(3))
    for d in range(1, NZ):
        f = at_z(d)
        landed(G.at[x, f], gs.at[0, d], gr.at[x, f], {"z": f})
    for d in range(1, NX):
        send(G.at[x], G.at[x], gs.at[1, d], yr.at[0, x], {"x": at_x(d)})
    x_stage(5)
    x_stage(4)
    CS[...] = neg_bar_one
    W[...] = H[...] * neg_bar_one
    yn = -row_all(3, row_pass(), total)
    Y[x, z, 0:1] = yn[:, :128]
    Y[x, z, 1:2] = yn[:, 128:]
    for d in range(1, NZ):
        send(Y.at[x, z], Y.at[x, z], ys.at[0, d], gr.at[NX + x, z], {"z": at_z(d)})
    XB[...] = XB[...] * -(N_B / N_K)
    FB[...] = spread(yn)
    CM[...] = jnp.exp2(CM[...]) * N_B
    RP[...] = jnp.zeros((ROWS, D), F32)

    def adjoint_rows(q, n):
        for b in range(8):
            at = slice(b * 32, (b + 1) * 32)
            ub, xb, yb = UB[at, :], XB[at, :], FB[at, :]
            for j in range(8):
                t = 8 * q + j
                g = ub * A[pl.ds(t, 1), :] + xb * H[pl.ds(t, 1), :]
                g = g + (yb * CM[pl.ds(t, 1), :] + W[pl.ds(t, 1), :])
                ADJ[n, at, j * 128:(j + 1) * 128] = (S[t, at, :] * g).astype(BF16)

    def row_grad(q, n):
        at = pl.multiple_of(q * 1024, 1024)
        RP[...] += jnp.dot(ADJ[n], PV[pl.ds(at, 1024), :], preferred_element_type=F32)

    def grad_chunk(q, _):
        row_grad(2 * q - 1, 1)
        adjoint_rows(2 * q, 0)
        row_grad(2 * q, 0)
        adjoint_rows(2 * q + 1, 1)
        return 0

    adjoint_rows(0, 0)
    row_grad(0, 0)
    adjoint_rows(1, 1)
    half = COLS // 4096
    lax.fori_loop(1, half, grad_chunk, 0)
    for d in range(1, NZ):
        f = at_z(d)
        landed(Y.at[x, f], ys.at[0, d], gr.at[NX + x, f], {"z": f})
    for d in range(1, NX):
        send(Y.at[x], Y.at[x], ys.at[1, d], yr.at[1, x], {"x": at_x(d)})
    lax.fori_loop(half, 2 * half, grad_chunk, 0)
    row_grad(4 * half - 1, 1)
    piece = ROWS // NY

    def quarter(j):
        return RP.at[pl.ds(pl.multiple_of(j * piece, piece), piece)]

    for d in range(1, NY):
        f = at_y(d)
        send(quarter(f), EB.at[y], eb_s.at[d], eb_r.at[y], {"p": f})
    EB[y] = quarter(y)[...]

    chip = x * NZ + z
    pown = PV.at[pl.ds(pl.multiple_of(chip * 512, 512), 512)]
    for j in range(4):
        at = pl.ds(j * 128, 128)
        line = pl.ds(chip * 4 + j, 1)
        LB[at, :] = spread(LG[line, :])
        AB[at, :] = spread(V[line, :])
        CB[at, :] = spread(CS[line, :])
        DB[at, :] = spread(jnp.exp2(LG[line, :]) * N_B)
    PG[...] = jnp.zeros((2 * ROWS, D), F32)
    for d in range(1, NX):
        f = at_x(d)
        landed(G.at[f], gs.at[1, d], yr.at[0, f], {"x": f})
        landed(Y.at[f], ys.at[1, d], yr.at[1, f], {"x": f})
        for r in range(NZ):
            zb = at_z(r)
            landed(EA.at[f, zb], es_x.at[r, d], er.at[f, zb], {"x": f})

    def back_scores(o, n):
        s = dot_nt(pown[...], EA[o // NZ, o % NZ]) * SCALE2
        ST[n] = s

    def back_adjoint(o, n, m):
        xb, zb = o // NZ, o % NZ
        for b in range(16):
            at = slice(b * 32, (b + 1) * 32)
            l, a, g0, d = LB[at, :], AB[at, :], CB[at, :], DB[at, :]
            for i in range(2):
                to = slice(i * 128, (i + 1) * 128)
                e = jnp.exp2((ST[n, at, to] - l) + G[xb, zb, i:i + 1])
                g = (a * G[xb, zb, 2 + i:3 + i] + G[xb, zb, 4 + i:5 + i]) + (g0 + d * Y[xb, zb, i:i + 1])
                ADJ2[m, at, (n % 2) * 256 + i * 128:(n % 2) * 256 + (i + 1) * 128] = (e * g).astype(BF16)

    def back_grad(o, m):
        rows = EA[o // NZ, pl.ds(o % NZ, 2)].reshape(2 * ROWS, D)
        PG[...] += jnp.dot(ADJ2[m], rows, preferred_element_type=F32)

    def back_four(q, first):
        o = 4 * q
        if not first:
            back_grad(o - 2, 1)
        back_scores(o + 1, 1)
        back_adjoint(o, 0, 0)
        back_scores(o + 2, 2)
        back_adjoint(o + 1, 1, 0)
        back_grad(o, 0)
        back_scores(o + 3, 3)
        back_adjoint(o + 2, 2, 1)
        back_scores(jnp.minimum(o + 4, NX * NZ - 1), 0)
        back_adjoint(o + 3, 3, 1)

    def back_block(q, _):
        back_four(q, False)
        return 0

    mid = NX * NZ // 8
    back_scores(0, 0)
    back_four(0, True)
    lax.fori_loop(1, mid, back_block, 0)
    for d in range(1, NY):
        f = at_y(d)
        landed(EB.at[f], eb_s.at[d], eb_r.at[f], {"p": f})
    EO[y] = total([EB[j] for j in range(NY)]) * SCALE
    for d in range(1, NY):
        send(EO.at[y], EO.at[y], eo_s.at[d], eo_r.at[y], {"p": at_y(d)})
    lax.fori_loop(mid, 2 * mid, back_block, 0)
    back_grad(NX * NZ - 2, 1)
    there = PG.at[pl.ds(pl.multiple_of((1 - c) * ROWS, ROWS), ROWS)]
    send(there, PR, pr_s, pr_r, {"c": 1 - c})
    for d in range(1, NY):
        f = at_y(d)
        landed(EO.at[f], eo_s.at[d], eo_r.at[f], {"p": f})
    eg_ref[...] = EO[...].reshape(ROWS, D)
    landed(PR, pr_s, pr_r, {"c": 1 - c})
    pg_ref[...] = (PG[pl.ds(pl.multiple_of(c * ROWS, ROWS), ROWS), :] + PR[...]) * SCALE
    for copy in sent:
        copy.wait_send()


def step(embeddings, prototypes, row_cot, col_cot):
    vm = pltpu.VMEM
    dma = pltpu.SemaphoreType.DMA
    wide = vm((ROWS, 128), F32)
    line = vm((TILES, 128), F32)
    scratch = [
        vm((TILES, ROWS, 128), F32), vm((COLS, D), BF16), vm((NX, NZ, ROWS, D), BF16),
        wide, wide, wide, wide,
        line, line, line, line, line, line, line,
        vm((2, ROWS, 1024), BF16), vm((ROWS, D), F32), vm((2 * ROWS, D), F32), vm((ROWS, D), F32),
        vm((512, 128), F32), vm((512, 128), F32), vm((512, 128), F32), vm((512, 128), F32), vm((2, 512, 512), BF16), vm((4, 512, ROWS), F32), vm((2, ROWS, 512), F32),
        vm((4, NY, 1, ROWS), F32), vm((3, 8, TILES // 8, 128), F32), vm((3, 8, TILES // 8, 128), F32),
        vm((3, NZ, TILES // 8, 128), F32), vm((3, 8, TILES // 8, 128), F32),
        vm((NX, NZ, 8, 128), F32), vm((NX, NZ, 2, 128), F32),
        vm((NY, ROWS // NY, D), F32), vm((NY, ROWS // NY, D), F32),
        dma((8,)), dma(()), dma((4, NY)), dma((4, NY)),
        dma((3, 8)), dma((3, 8)), dma((3, 8)), dma((3, 8)), dma((3, 8)), dma((3, 8)),
        dma((NZ,)), dma((NZ, NX)), dma((NX, NZ)), dma((2, NZ)), dma((2 * NX, NZ)),
        dma((2, NZ)), dma((2, NX)),
        dma((NY,)), dma((NY,)), dma((NY,)), dma((NY,)), dma(()), dma(()),
    ]
    anywhere = pl.BlockSpec(memory_space=pl.ANY)
    inside = pl.BlockSpec(memory_space=pltpu.VMEM)
    return pl.pallas_call(
        kernel,
        out_shape=(jax.ShapeDtypeStruct((ROWS, D), F32), jax.ShapeDtypeStruct((ROWS, D), F32)),
        in_specs=[anywhere, anywhere, inside, inside],
        out_specs=(inside, inside),
        scratch_shapes=scratch,
        compiler_params=pltpu.CompilerParams(collective_id=0, has_side_effects=True, vmem_limit_bytes=60 << 20),
        name="sinkhorn_back",
    )(embeddings, prototypes, row_cot.reshape(1, ROWS), col_cot.reshape(TILES, 128))


def solution(mesh):
    split = Mesh(mesh.devices.reshape(NX, NZ, NC, NY), ("x", "z", "c", "p"))
    rows = ("x", "z", "c")
    return jax.shard_map(
        step,
        mesh=split,
        in_specs=(P(rows, None), P("p", None), P(rows), P("p")),
        out_specs=(P(rows, None), P(("p",) + rows, None)),
        check_vma=False,
    )
```

```python
import math

import jax
import jax.numpy as jnp
from jax import lax
from jax.experimental import pallas as pl
from jax.experimental.pallas import tpu as pltpu
from jax.sharding import Mesh
from jax.sharding import PartitionSpec as P

MESH = pl.DeviceIdType.MESH
LOG2E = math.log2(math.e)
SCALE = 4.0
SCALE2 = SCALE * LOG2E
F32 = jnp.float32
BF16 = jnp.bfloat16
NX, NZ, NC, NY = 4, 8, 2, 4
ROWS, COLS, WIDTH = 256, 16384, 256
TILES = COLS // 128
GROUP = TILES // 8
FAR_FIRST = ((2, 0), (2, 1), (1, 0), (1, 1), (3, 0), (3, 1), (0, 1))
LOG2_B = math.log2(ROWS * NX * NZ * NC)
N_B = float(ROWS * NX * NZ * NC)
N_K = float(COLS * NY)


def dot_nt(a, b):
    return lax.dot_general(a, b, (((1,), (1,)), ((), ())), preferred_element_type=F32)


def lse2(parts):
    top = parts[0]
    for p in parts[1:]:
        top = jnp.maximum(top, p)
    mass = jnp.exp2(parts[0] - top)
    for p in parts[1:]:
        mass = mass + jnp.exp2(p - top)
    return top + jnp.log(mass) * LOG2E


def total(parts):
    out = parts[0]
    for p in parts[1:]:
        out = out + p
    return out


def row_form(acc):
    return jnp.sum(acc.T, axis=0, keepdims=True)


def spread(row):
    return jnp.broadcast_to(row, (128, row.shape[1])).T


def kernel(emb_hbm, protos_hbm, rcot_ref, ccot_ref, eg_ref, pg_ref,
           S, PV, EA, MX, FB, UB, XB, CM, CS, W, D, NB, LG, V, ADJ, RP, PG, PR, LB, AB, CB, DB, ADJ2, NP, T,
           rbuf, cloc, c1, c2, c3, G, Y, FG, EB, EO,
           psem, esem, rs, rr, s1, r1, s2, r2, s3, r3, es_z, es_x, es_y, er, gs, gr, ys, yr, fs, fr, eb_s, eb_r, eo_s, eo_r, pr_s, pr_r):
    x, z, c, y = lax.axis_index("x"), lax.axis_index("z"), lax.axis_index("c"), lax.axis_index("p")
    k = x * NC + c
    sent = []

    def send(src, dst, ssem, rsem, where):
        copy = pltpu.make_async_remote_copy(src_ref=src, dst_ref=dst, send_sem=ssem, recv_sem=rsem,
                                            device_id=where, device_id_type=MESH)
        copy.start()
        sent.append(copy)

    def landed(ref, ssem, rsem, where):
        pltpu.make_async_remote_copy(src_ref=ref, dst_ref=ref, send_sem=ssem, recv_sem=rsem,
                                     device_id=where, device_id_type=MESH).wait_recv()

    def at_y(d):
        return (y + d % NY) % NY

    def at_z(d):
        return (z + d) % NZ

    def at_x(d):
        return (x + d) % NX

    def at_k(d):
        return (k + d) % (NX * NC)

    def xc(kk):
        return {"x": kk // NC, "c": kk % NC}

    barrier = pltpu.get_barrier_semaphore()
    for d in range(1, NY):
        pl.semaphore_signal(barrier, inc=1, device_id={"p": at_y(d)}, device_id_type=MESH)
    for d in range(1, NX * NC):
        pl.semaphore_signal(barrier, inc=1, device_id=xc(at_k(d)), device_id_type=MESH)
    for d in range(1, NZ):
        pl.semaphore_signal(barrier, inc=1, device_id={"z": at_z(d)}, device_id_type=MESH)

    own = pltpu.make_async_copy(emb_hbm, EA.at[x, z], esem)
    own.start()
    step = COLS // 8
    loads = [pltpu.make_async_copy(protos_hbm.at[pl.ds(q * step, step)], PV.at[pl.ds(q * step, step)], psem.at[q])
             for q in range(8)]
    for q in loads:
        q.start()
    MX[...] = jnp.full((ROWS, 128), -jnp.inf, F32)
    own.wait()

    def fold(q, n):
        for b in range(4):
            at = slice(b * 64, (b + 1) * 64)
            tiles = [T[n, at, j * 128:(j + 1) * 128] for j in range(4)]
            old = MX[at, :]
            new = jnp.maximum(jnp.maximum(jnp.maximum(tiles[0], tiles[1]), jnp.maximum(tiles[2], tiles[3])), old)
            mass = XB[at, :] * jnp.exp2(old - new)
            more = (jnp.exp2(tiles[0] - new) + jnp.exp2(tiles[1] - new)) + (jnp.exp2(tiles[2] - new) + jnp.exp2(tiles[3] - new))
            XB[at, :] = mass + more
            MX[at, :] = new
            for j in range(4):
                S[4 * q + j, at, :] = tiles[j]

    def score(q, n):
        at = pl.multiple_of(q * 512, 512)
        T[n] = dot_nt(EA[x, z], PV[pl.ds(at, 512), :]) * SCALE2

    def score_chunk(q, _):
        score(2 * q + 1, 1)
        fold(2 * q, 0)
        score(jnp.minimum(2 * q + 2, TILES // 4 - 1), 0)
        fold(2 * q + 1, 1)
        return 0

    parity = y % 2

    def offset(n, p):
        return (p, 2 + 5 * p, 6 - 3 * p, 4 + p)[n]

    def z_copy(n, there):
        return pltpu.make_async_remote_copy(
            src_ref=EA.at[x, z], dst_ref=EA.at[x, z], send_sem=es_z.at[n], recv_sem=er.at[x, z],
            device_id={"z": there}, device_id_type=MESH)

    def z_stage(n):
        there = at_z(NZ - offset(n, parity))
        if n:
            z_copy(n, there).start()
        else:
            @pl.when(parity == 1)
            def _():
                z_copy(n, there).start()

    def z_landed(n):
        f = at_z(offset(n, parity))
        if n:
            landed(EA.at[x, f], es_z.at[n], er.at[x, f], {"z": f})
        else:
            @pl.when(parity == 1)
            def _():
                landed(EA.at[x, f], es_z.at[n], er.at[x, f], {"z": f})

    def z_sent(n):
        if n:
            z_copy(n, at_z(1)).wait_send()
        else:
            @pl.when(parity == 1)
            def _():
                z_copy(n, at_z(1)).wait_send()

    def x_stage(n):
        z_landed(n)
        zb = at_z(offset(n, parity))
        for d in range(1, NX):
            send(EA.at[x, zb], EA.at[x, zb], es_x.at[n, d], er.at[x, zb], {"x": at_x(d)})

    def y_first(zb):
        return pltpu.make_async_remote_copy(
            src_ref=EA.at[x, zb], dst_ref=EA.at[x, zb], send_sem=es_y.at[0, 0], recv_sem=er.at[x, zb],
            device_id={"p": at_y(1)}, device_id_type=MESH)

    def y_stage(n):
        zb = at_z(offset(n, parity))
        if n:
            send(EA.at[x, zb], EA.at[x, zb], es_y.at[n, 0], er.at[x, zb], {"p": at_y(1)})
        else:
            @pl.when(parity == 1)
            def _():
                y_first(zb).start()

        for d in range(1, NX):
            f = at_x(d)
            landed(EA.at[f, zb], es_x.at[n, d], er.at[f, zb], {"x": f})
            send(EA.at[f, zb], EA.at[f, zb], es_y.at[n, d], er.at[f, zb], {"p": at_y(1 if d < 2 else -1)})

    XB[...] = jnp.zeros((ROWS, 128), F32)
    loads[0].wait()
    score(0, 0)

    def part(q, _):
        pltpu.make_async_copy(protos_hbm.at[pl.ds(q * step, step)], PV.at[pl.ds(q * step, step)], psem.at[q]).wait()
        lax.fori_loop(q * 2 - 2, q * 2, score_chunk, 0)
        return 0

    lax.fori_loop(1, 4, part, 0)
    pl.semaphore_wait(barrier, NY - 1 + NX * NC - 1 + NZ - 1)
    for n in range(4):
        z_stage(n)
    lax.fori_loop(4, 8, part, 0)
    x_stage(0)
    lax.fori_loop(14, 16, score_chunk, 0)
    mt = MX[...].T
    top = jnp.max(mt, axis=0, keepdims=True)
    loc = top + jnp.log(jnp.sum(XB[...].T * jnp.exp2(mt - top), axis=0, keepdims=True)) * LOG2E

    def row_all(i, row, combine, fill):
        rbuf[i, y] = row
        for d in range(1, NY):
            send(rbuf.at[i, y], rbuf.at[i, y], rs.at[i, d], rr.at[i, y], {"p": at_y(d)})
        fill()
        for d in range(1, NY):
            f = at_y(d)
            landed(rbuf.at[i, f], rs.at[i, d], rr.at[i, f], {"p": f})
        return combine([rbuf[i, j] for j in range(NY)])

    def peers():
        for j, (dx, dc) in enumerate(FAR_FIRST):
            xx, cc = at_x(dx), (c + dc) % NC
            yield j, xx * NC + cc, {"x": xx, "c": cc}

    def col_round(i, piece, combine, fill_one, fill_two, use):
        for j, f, where in peers():
            cloc[i, f] = piece(f)
            send(cloc.at[i, f], c1.at[i, k], s1.at[i, j], r1.at[i, k], where)
        c1[i, k] = piece(k)
        fill_one()
        for j, f, where in peers():
            landed(c1.at[i, f], s1.at[i, j], r1.at[i, f], where)
        c2[i, z] = combine([c1[i, j] for j in range(8)])
        for d in range(1, NZ):
            send(c2.at[i, z], c2.at[i, z], s2.at[i, d], r2.at[i, z], {"z": at_z(d)})
        fill_two()
        for d in range(1, NZ):
            f = at_z(d)
            landed(c2.at[i, f], s2.at[i, d], r2.at[i, f], {"z": f})
        c3[i, k] = combine([c2[i, j] for j in range(NZ)])
        for j, f, where in peers():
            send(c3.at[i, k], c3.at[i, k], s3.at[i, j], r3.at[i, k], where)
        MX[...] = jnp.zeros((ROWS, 128), F32)
        use(k, c3[i, k])
        for j, f, where in list(peers())[::-1]:
            landed(c3.at[i, f], s3.at[i, j], r3.at[i, f], where)
            use(f, c3[i, f])
        return row_form(MX[...])

    def group(f):
        return pl.ds(pl.multiple_of(f * GROUP, GROUP), GROUP)

    def row_add(f, keep):
        def block(b, _):
            at = pl.ds(pl.multiple_of(b * 64, 64), 64)
            acc = [MX[at, :], jnp.zeros((64, 128), F32)]
            for j in range(GROUP):
                t = f * GROUP + j
                term = S[t, at, :] * W[pl.ds(t, 1), :]
                if keep:
                    S[t, at, :] = term
                acc[j % 2] = acc[j % 2] + term
            MX[at, :] = acc[0] + acc[1]
            return 0
        lax.fori_loop(0, 4, block, 0)

    def col_piece(weights, f):
        def tile(q, _):
            t = f * GROUP + 4 * q
            acc = [None] * 4
            for b in range(4):
                at = slice(b * 64, (b + 1) * 64)
                w = weights[at, :]
                for j in range(4):
                    term = S[t + j, at, :] * w
                    acc[j] = term if b == 0 else acc[j] + term
            for j in range(4):
                CS[pl.ds(t + j, 1), :] = jnp.sum(acc[j], axis=0, keepdims=True)
            return 0
        lax.fori_loop(0, GROUP // 4, tile, 0)
        return CS[group(f), :]

    def bulk_one():
        pass

    f_one = -LOG2_B - row_all(0, loc, lse2, bulk_one)
    FB[...] = spread(f_one)
    FG[x, z, 0:1] = f_one[:, :128]
    FG[x, z, 1:2] = f_one[:, 128:]
    for d in range(1, NZ):
        send(FG.at[x, z], FG.at[x, z], fs.at[0, d], fr.at[0, z], {"z": at_z(d)})

    def tops(t):
        best = [None, None]
        for b in range(4):
            at = slice(b * 64, (b + 1) * 64)
            f = FB[at, :]
            for j in range(2):
                here = S[t + j, at, :] + f
                best[j] = here if b == 0 else jnp.maximum(best[j], here)
        return tuple(jnp.max(m, axis=0, keepdims=True) for m in best)

    def plan_piece(f):
        start = f * GROUP

        def tile(q, m):
            t = start + 2 * q
            later = tops(jnp.minimum(t + 2, start + GROUP - 2))
            acc = [None, None]
            for b in range(4):
                at = slice(b * 64, (b + 1) * 64)
                fb = FB[at, :]
                for j in range(2):
                    e = jnp.exp2(S[t + j, at, :] + fb - m[j])
                    S[t + j, at, :] = e
                    acc[j] = e if b == 0 else acc[j] + e
            for j in range(2):
                CM[pl.ds(t + j, 1), :] = m[j]
                CS[pl.ds(t + j, 1), :] = jnp.sum(acc[j], axis=0, keepdims=True)
            return later

        lax.fori_loop(0, GROUP // 2, tile, tops(start))
        at = group(f)
        return CM[at, :] + jnp.log(CS[at, :]) * LOG2E

    chip = x * NZ + z
    pown = PV.at[pl.ds(pl.multiple_of(chip * 512, 512), 512)]

    def own_cols(ref, out):
        for j in range(4):
            out[j * 128:(j + 1) * 128, :] = spread(ref[pl.ds(chip * 4 + j, 1), :])

    def back_plan(n, theirs):
        zb = at_z(offset(n, 1 - parity if theirs else parity))
        if theirs:
            if n == 0:
                @pl.when(parity == 0)
                def _():
                    y_first(zb).wait_recv()

            for d in range(1 if n == 0 else 0, NX):
                f = at_x(d)
                landed(EA.at[f, zb], es_y.at[n, d], er.at[f, zb], {"p": at_y(-1 if d < 2 else 1)})

        def block(xb, _):
            s = dot_nt(pown[...], EA[xb, zb]) * SCALE2
            for i in range(2):
                NP[xb * NZ + zb, :, i * 128:(i + 1) * 128] = jnp.exp2(
                    (s[:, i * 128:(i + 1) * 128] - LB[...]) + FG[xb, zb, i:i + 1])
            return 0

        lax.fori_loop(0, NX, block, 0)

    def share_f():
        y_stage(0)
        for d in range(1, NZ):
            f = at_z(d)
            landed(FG.at[x, f], fs.at[0, d], fr.at[0, f], {"z": f})
        for d in range(1, NX):
            send(FG.at[x], FG.at[x], fs.at[1, d], fr.at[1, x], {"x": at_x(d)})

    def use_one(f, big):
        at = group(f)
        LG[at, :] = big
        D[at, :] = jnp.exp2(big) * N_B
        W[at, :] = jnp.exp2(CM[at, :] - big)
        row_add(f, True)

    def fill_row_two():
        x_stage(2)
        own_cols(LG, LB)
        for d in range(1, NX):
            f = at_x(d)
            landed(FG.at[f], fs.at[1, d], fr.at[1, f], {"x": f})
        back_plan(0, False)

    mass = col_round(0, plan_piece, lse2, share_f, lambda: x_stage(1), use_one)
    u = (N_K / N_B) / row_all(1, mass, total, fill_row_two)
    UB[...] = spread(u)

    def use_two(f, col):
        at = group(f)
        V[at, :] = ccot_ref[at, :] * (-1.0 / col)
        W[at, :] = V[at, :]
        row_add(f, False)

    def fill_col_two():
        x_stage(3)
        y_stage(2)
        back_plan(0, True)

    def fill_row_three():
        own_cols(V, AB)
        back_plan(2, False)

    def fill_col_two_first():
        y_stage(1)
        back_plan(1, False)

    moved = col_round(1, lambda f: col_piece(UB, f), total, fill_col_two_first, fill_col_two, use_two)
    bar_two = rcot_ref[...] + u * row_all(2, moved, total, fill_row_three)
    xr = bar_two * u
    XB[...] = spread(xr)
    xn = xr * -(N_B / N_K)
    for j, vec in enumerate((u, xn)):
        G[x, z, 2 * j:2 * j + 1] = vec[:, :128]
        G[x, z, 2 * j + 1:2 * j + 2] = vec[:, 128:]
    for d in range(1, NZ):
        send(G.at[x, z], G.at[x, z], gs.at[0, d], gr.at[x, z], {"z": at_z(d)})

    def use_three(f, col):
        at = group(f)
        NB[at, :] = col * (N_B / N_K)
        W[at, :] = NB[at, :]
        row_add(f, False)

    def fill_col_three():
        for d in range(1, NZ):
            f = at_z(d)
            landed(G.at[x, f], gs.at[0, d], gr.at[x, f], {"z": f})
        for d in range(1, NX):
            send(G.at[x], G.at[x], gs.at[1, d], yr.at[0, x], {"x": at_x(d)})
        back_plan(3, False)
        back_plan(2, True)

    def fill_row_four():
        XB[...] = XB[...] * -(N_B / N_K)
        own_cols(NB, CB)
        own_cols(D, DB)
        back_plan(3, True)

    def fill_col_three_first():
        y_stage(3)
        back_plan(1, True)

    last = col_round(2, lambda f: col_piece(XB, f), total, fill_col_three_first, fill_col_three, use_three)
    yn = -row_all(3, last, total, fill_row_four)
    Y[x, z, 0:1] = yn[:, :128]
    Y[x, z, 1:2] = yn[:, 128:]
    for d in range(1, NZ):
        send(Y.at[x, z], Y.at[x, z], ys.at[0, d], gr.at[NX + x, z], {"z": at_z(d)})
    FB[...] = spread(yn)
    RP[...] = jnp.zeros((ROWS, WIDTH), F32)

    HALF = ROWS // 2
    piece = ROWS // NY

    def adjoint_rows(q, n, h):
        for b in range(4):
            at = slice(h * HALF + b * 32, h * HALF + (b + 1) * 32)
            ub, xb, yb = UB[at, :], XB[at, :], FB[at, :]
            for j in range(8):
                t = 8 * q + j
                g = (ub * V[pl.ds(t, 1), :] + xb) + (yb * D[pl.ds(t, 1), :] + NB[pl.ds(t, 1), :])
                ADJ[n, b * 32:(b + 1) * 32, j * 128:(j + 1) * 128] = (S[t, at, :] * g).astype(BF16)

    def row_grad(q, n, h):
        at = pl.multiple_of(q * 1024, 1024)
        rows = slice(h * HALF, (h + 1) * HALF)
        RP[rows, :] += jnp.dot(ADJ[n], PV[pl.ds(at, 1024), :], preferred_element_type=F32)

    def grad_half(h):
        def grad_chunk(q, _):
            row_grad(2 * q - 1, 1, h)
            adjoint_rows(2 * q, 0, h)
            row_grad(2 * q, 0, h)
            adjoint_rows(2 * q + 1, 1, h)
            return 0

        adjoint_rows(0, 0, h)
        row_grad(0, 0, h)
        adjoint_rows(1, 1, h)
        lax.fori_loop(1, COLS // 2048, grad_chunk, 0)
        row_grad(COLS // 1024 - 1, 1, h)
        for j in range(2 * h, 2 * h + 2):
            EB[j, y] = RP[j * piece:(j + 1) * piece, :]

            @pl.when(y != j)
            def _():
                eb_copy(j).start()

    def eb_copy(j):
        return pltpu.make_async_remote_copy(
            src_ref=EB.at[j, y], dst_ref=EB.at[j, y], send_sem=eb_s.at[j], recv_sem=eb_r.at[y],
            device_id={"p": j}, device_id_type=MESH)

    grad_half(0)
    for d in range(1, NZ):
        f = at_z(d)
        landed(Y.at[x, f], ys.at[0, d], gr.at[NX + x, f], {"z": f})
    for d in range(1, NX):
        send(Y.at[x], Y.at[x], ys.at[1, d], yr.at[1, x], {"x": at_x(d)})
    grad_half(1)

    PG[...] = jnp.zeros((2 * ROWS, WIDTH), F32)
    for d in range(1, NX):
        f = at_x(d)
        landed(G.at[f], gs.at[1, d], yr.at[0, f], {"x": f})
        landed(Y.at[f], ys.at[1, d], yr.at[1, f], {"x": f})

    def back_adjoint(o, n, m):
        xb, zb = o // NZ, o % NZ
        for b in range(16):
            at = slice(b * 32, (b + 1) * 32)
            a, g0, d = AB[at, :], CB[at, :], DB[at, :]
            for i in range(2):
                g = (a * G[xb, zb, i:i + 1] + G[xb, zb, 2 + i:3 + i]) + (g0 + d * Y[xb, zb, i:i + 1])
                to = slice(n * 256 + i * 128, n * 256 + (i + 1) * 128)
                ADJ2[m, at, to] = (NP[o, at, i * 128:(i + 1) * 128] * g).astype(BF16)

    def back_grad(o, m):
        rows = EA[o // NZ, pl.ds(o % NZ, 2)].reshape(2 * ROWS, WIDTH)
        PG[...] += jnp.dot(ADJ2[m], rows, preferred_element_type=F32)

    def back_block(q, _):
        o = 4 * q
        back_grad(o - 2, 1)
        back_adjoint(o, 0, 0)
        back_adjoint(o + 1, 1, 0)
        back_grad(o, 0)
        back_adjoint(o + 2, 0, 1)
        back_adjoint(o + 3, 1, 1)
        return 0

    def share_rows():
        for d in range(1, NY):
            f = at_y(d)
            landed(EB.at[y, f], eb_s.at[0], eb_r.at[f], {"p": f})
        EO[y] = total([EB[y, j] for j in range(NY)]) * SCALE
        for d in range(1, NY):
            send(EO.at[y], EO.at[y], eo_s.at[d], eo_r.at[y], {"p": at_y(d)})

    back_adjoint(0, 0, 0)
    back_adjoint(1, 1, 0)
    back_grad(0, 0)
    back_adjoint(2, 0, 1)
    back_adjoint(3, 1, 1)
    lax.fori_loop(1, 4, back_block, 0)
    share_rows()
    lax.fori_loop(4, NX * NZ // 4, back_block, 0)
    back_grad(NX * NZ - 2, 1)
    there = PG.at[pl.ds(pl.multiple_of((1 - c) * ROWS, ROWS), ROWS)]
    send(there, PR, pr_s, pr_r, {"c": 1 - c})
    for d in range(1, NY):
        f = at_y(d)
        landed(EO.at[f], eo_s.at[d], eo_r.at[f], {"p": f})
    eg_ref[...] = EO[...].reshape(ROWS, WIDTH)
    landed(PR, pr_s, pr_r, {"c": 1 - c})
    pg_ref[...] = (PG[pl.ds(pl.multiple_of(c * ROWS, ROWS), ROWS), :] + PR[...]) * SCALE
    @pl.when(parity == 1)
    def _():
        y_first(z).wait_send()

    for n in range(4):
        z_sent(n)

        @pl.when(y != n)
        def _():
            eb_copy(n).wait_send()
    for copy in sent:
        copy.wait_send()


def step(embeddings, prototypes, row_cot, col_cot):
    vm = pltpu.VMEM
    dma = pltpu.SemaphoreType.DMA
    wide = vm((ROWS, 128), F32)
    line = vm((TILES, 128), F32)
    scratch = [
        vm((TILES, ROWS, 128), F32), vm((COLS, WIDTH), BF16), vm((NX, NZ, ROWS, WIDTH), BF16),
        wide, wide, wide, wide,
        line, line, line, line, line, line, line,
        vm((2, ROWS // 2, 1024), BF16), vm((ROWS, WIDTH), F32), vm((2 * ROWS, WIDTH), F32), vm((ROWS, WIDTH), F32),
        vm((512, 128), F32), vm((512, 128), F32), vm((512, 128), F32), vm((512, 128), F32), vm((2, 512, 512), BF16), vm((NX * NZ, 512, ROWS), F32), vm((2, ROWS, 512), F32),
        vm((4, NY, 1, ROWS), F32), vm((3, 8, TILES // 8, 128), F32), vm((3, 8, TILES // 8, 128), F32),
        vm((3, NZ, TILES // 8, 128), F32), vm((3, 8, TILES // 8, 128), F32),
        vm((NX, NZ, 4, 128), F32), vm((NX, NZ, 2, 128), F32), vm((NX, NZ, 2, 128), F32),
        vm((NY, NY, ROWS // NY, WIDTH), F32), vm((NY, ROWS // NY, WIDTH), F32),
        dma((8,)), dma(()), dma((4, NY)), dma((4, NY)),
        dma((3, 8)), dma((3, 8)), dma((3, 8)), dma((3, 8)), dma((3, 8)), dma((3, 8)),
        dma((4,)), dma((4, NX)), dma((4, NX)), dma((NX, NZ)), dma((2, NZ)), dma((2 * NX, NZ)),
        dma((2, NZ)), dma((2, NX)), dma((2, NZ)), dma((2, NZ)),
        dma((NY,)), dma((NY,)), dma((NY,)), dma((NY,)), dma(()), dma(()),
    ]
    anywhere = pl.BlockSpec(memory_space=pl.ANY)
    inside = pl.BlockSpec(memory_space=pltpu.VMEM)
    return pl.pallas_call(
        kernel,
        out_shape=(jax.ShapeDtypeStruct((ROWS, WIDTH), F32), jax.ShapeDtypeStruct((ROWS, WIDTH), F32)),
        in_specs=[anywhere, anywhere, inside, inside],
        out_specs=(inside, inside),
        scratch_shapes=scratch,
        compiler_params=pltpu.CompilerParams(collective_id=0, has_side_effects=True, vmem_limit_bytes=60 << 20),
        name="sinkhorn_back",
    )(embeddings, prototypes, row_cot.reshape(1, ROWS), col_cot.reshape(TILES, 128))


def solution(mesh):
    split = Mesh(mesh.devices.reshape(NX, NZ, NC, NY), ("x", "z", "c", "p"))
    rows = ("x", "z", "c")
    return jax.shard_map(
        step,
        mesh=split,
        in_specs=(P(rows, None), P("p", None), P(rows), P("p")),
        out_specs=(P(rows, None), P(("p",) + rows, None)),
        check_vma=False,
    )
```

```python
import math

import jax
import jax.numpy as jnp
from jax import lax
from jax.experimental import pallas as pl
from jax.experimental.pallas import tpu as pltpu
from jax.sharding import Mesh
from jax.sharding import PartitionSpec as P

MESH = pl.DeviceIdType.MESH
LOG2E = math.log2(math.e)
SCALE = 4.0
SCALE2 = SCALE * LOG2E
F32 = jnp.float32
BF16 = jnp.bfloat16
NX, NZ, NC, NY = 4, 8, 2, 4
ROWS, COLS, WIDTH = 256, 16384, 256
TILES = COLS // 128
GROUP = TILES // 8
FAR_FIRST = ((2, 0), (2, 1), (1, 0), (1, 1), (3, 0), (3, 1), (0, 1))
LOG2_B = math.log2(ROWS * NX * NZ * NC)
N_B = float(ROWS * NX * NZ * NC)
N_K = float(COLS * NY)


def dot_nt(a, b):
    return lax.dot_general(a, b, (((1,), (1,)), ((), ())), preferred_element_type=F32)


def lse2(parts):
    top = parts[0]
    for p in parts[1:]:
        top = jnp.maximum(top, p)
    mass = jnp.exp2(parts[0] - top)
    for p in parts[1:]:
        mass = mass + jnp.exp2(p - top)
    return top + jnp.log(mass) * LOG2E


def total(parts):
    out = parts[0]
    for p in parts[1:]:
        out = out + p
    return out


def row_form(acc):
    return jnp.sum(acc.T, axis=0, keepdims=True)


def spread(row):
    return jnp.broadcast_to(row, (128, row.shape[1])).T


def kernel(emb_hbm, protos_hbm, rcot_ref, ccot_ref, eg_ref, pg_ref,
           S, PV, EA, MX, FB, UB, XB, CM, CS, W, D, NB, LG, V, ADJ, RP, PG, PR, LB, AB, CB, DB, ADJ2, NP, T,
           rbuf, cloc, c1, c2, c3, G, Y, FG, EB, EO,
           psem, esem, rs, rr, s1, r1, s2, r2, s3, r3, es_z, es_x, es_y, er, gs, gr, ys, yr, fs, fr, eb_s, eb_r, eo_s, eo_r, pr_s, pr_r):
    x, z, c, y = lax.axis_index("x"), lax.axis_index("z"), lax.axis_index("c"), lax.axis_index("p")
    k = x * NC + c
    sent = []

    def send(src, dst, ssem, rsem, where):
        copy = pltpu.make_async_remote_copy(src_ref=src, dst_ref=dst, send_sem=ssem, recv_sem=rsem,
                                            device_id=where, device_id_type=MESH)
        copy.start()
        sent.append(copy)

    def landed(ref, ssem, rsem, where):
        pltpu.make_async_remote_copy(src_ref=ref, dst_ref=ref, send_sem=ssem, recv_sem=rsem,
                                     device_id=where, device_id_type=MESH).wait_recv()

    def at_y(d):
        return (y + d % NY) % NY

    def at_z(d):
        return (z + d) % NZ

    def at_x(d):
        return (x + d) % NX

    def at_k(d):
        return (k + d) % (NX * NC)

    def xc(kk):
        return {"x": kk // NC, "c": kk % NC}

    barrier = pltpu.get_barrier_semaphore()
    for d in range(1, NY):
        pl.semaphore_signal(barrier, inc=1, device_id={"p": at_y(d)}, device_id_type=MESH)
    for d in range(1, NX * NC):
        pl.semaphore_signal(barrier, inc=1, device_id=xc(at_k(d)), device_id_type=MESH)
    for d in range(1, NZ):
        pl.semaphore_signal(barrier, inc=1, device_id={"z": at_z(d)}, device_id_type=MESH)

    own = pltpu.make_async_copy(emb_hbm, EA.at[x, z], esem)
    own.start()
    step = COLS // 8
    loads = [pltpu.make_async_copy(protos_hbm.at[pl.ds(q * step, step)], PV.at[pl.ds(q * step, step)], psem.at[q])
             for q in range(8)]
    for q in loads:
        q.start()
    MX[...] = jnp.full((ROWS, 128), -jnp.inf, F32)
    own.wait()

    def fold(q, n):
        for b in range(4):
            at = slice(b * 64, (b + 1) * 64)
            tiles = [T[n, at, j * 128:(j + 1) * 128] for j in range(4)]
            old = MX[at, :]
            new = jnp.maximum(jnp.maximum(jnp.maximum(tiles[0], tiles[1]), jnp.maximum(tiles[2], tiles[3])), old)
            mass = XB[at, :] * jnp.exp2(old - new)
            more = (jnp.exp2(tiles[0] - new) + jnp.exp2(tiles[1] - new)) + (jnp.exp2(tiles[2] - new) + jnp.exp2(tiles[3] - new))
            XB[at, :] = mass + more
            MX[at, :] = new
            for j in range(4):
                S[4 * q + j, at, :] = tiles[j]

    def score(q, n):
        at = pl.multiple_of(q * 512, 512)
        T[n] = dot_nt(EA[x, z], PV[pl.ds(at, 512), :]) * SCALE2

    def score_chunk(q, _):
        score(2 * q + 1, 1)
        fold(2 * q, 0)
        score(jnp.minimum(2 * q + 2, TILES // 4 - 1), 0)
        fold(2 * q + 1, 1)
        return 0

    parity = y % 2

    def offset(n, p):
        return (p, 2 + 5 * p, 6 - 3 * p, 4 + p)[n]

    def z_copy(n, there):
        return pltpu.make_async_remote_copy(
            src_ref=EA.at[x, z], dst_ref=EA.at[x, z], send_sem=es_z.at[n], recv_sem=er.at[x, z],
            device_id={"z": there}, device_id_type=MESH)

    def z_stage(n):
        there = at_z(NZ - offset(n, parity))
        if n:
            z_copy(n, there).start()
        else:
            @pl.when(parity == 1)
            def _():
                z_copy(n, there).start()

    def z_landed(n):
        f = at_z(offset(n, parity))
        if n:
            landed(EA.at[x, f], es_z.at[n], er.at[x, f], {"z": f})
        else:
            @pl.when(parity == 1)
            def _():
                landed(EA.at[x, f], es_z.at[n], er.at[x, f], {"z": f})

    def z_sent(n):
        if n:
            z_copy(n, at_z(1)).wait_send()
        else:
            @pl.when(parity == 1)
            def _():
                z_copy(n, at_z(1)).wait_send()

    def x_stage(n):
        z_landed(n)
        zb = at_z(offset(n, parity))
        for d in range(1, NX):
            send(EA.at[x, zb], EA.at[x, zb], es_x.at[n, d], er.at[x, zb], {"x": at_x(d)})

    def y_first(zb):
        return pltpu.make_async_remote_copy(
            src_ref=EA.at[x, zb], dst_ref=EA.at[x, zb], send_sem=es_y.at[0, 0], recv_sem=er.at[x, zb],
            device_id={"p": at_y(1)}, device_id_type=MESH)

    def y_stage(n):
        zb = at_z(offset(n, parity))
        if n:
            send(EA.at[x, zb], EA.at[x, zb], es_y.at[n, 0], er.at[x, zb], {"p": at_y(1)})
        else:
            @pl.when(parity == 1)
            def _():
                y_first(zb).start()

        for d in range(1, NX):
            f = at_x(d)
            landed(EA.at[f, zb], es_x.at[n, d], er.at[f, zb], {"x": f})
            send(EA.at[f, zb], EA.at[f, zb], es_y.at[n, d], er.at[f, zb], {"p": at_y(1 if d < 2 else -1)})

    XB[...] = jnp.zeros((ROWS, 128), F32)
    loads[0].wait()
    score(0, 0)

    def part(q, _):
        pltpu.make_async_copy(protos_hbm.at[pl.ds(q * step, step)], PV.at[pl.ds(q * step, step)], psem.at[q]).wait()
        lax.fori_loop(q * 2 - 2, q * 2, score_chunk, 0)
        return 0

    lax.fori_loop(1, 4, part, 0)
    pl.semaphore_wait(barrier, NY - 1 + NX * NC - 1 + NZ - 1)
    for n in range(4):
        z_stage(n)
    lax.fori_loop(4, 8, part, 0)
    x_stage(0)
    lax.fori_loop(14, 16, score_chunk, 0)
    mt = MX[...].T
    top = jnp.max(mt, axis=0, keepdims=True)
    loc = top + jnp.log(jnp.sum(XB[...].T * jnp.exp2(mt - top), axis=0, keepdims=True)) * LOG2E

    def row_all(i, row, combine, fill):
        rbuf[i, y] = row
        for d in range(1, NY):
            send(rbuf.at[i, y], rbuf.at[i, y], rs.at[i, d], rr.at[i, y], {"p": at_y(d)})
        fill()
        for d in range(1, NY):
            f = at_y(d)
            landed(rbuf.at[i, f], rs.at[i, d], rr.at[i, f], {"p": f})
        return combine([rbuf[i, j] for j in range(NY)])

    def peers():
        for j, (dx, dc) in enumerate(FAR_FIRST):
            xx, cc = at_x(dx), (c + dc) % NC
            yield j, xx * NC + cc, {"x": xx, "c": cc}

    def col_round(i, piece, combine, fill_one, fill_two, use):
        for j, f, where in peers():
            cloc[i, f] = piece(f)
            send(cloc.at[i, f], c1.at[i, k], s1.at[i, j], r1.at[i, k], where)
        c1[i, k] = piece(k)
        fill_one()
        for j, f, where in peers():
            landed(c1.at[i, f], s1.at[i, j], r1.at[i, f], where)
        c2[i, z] = combine([c1[i, j] for j in range(8)])
        for d in range(1, NZ):
            send(c2.at[i, z], c2.at[i, z], s2.at[i, d], r2.at[i, z], {"z": at_z(d)})
        fill_two()
        for d in range(1, NZ):
            f = at_z(d)
            landed(c2.at[i, f], s2.at[i, d], r2.at[i, f], {"z": f})
        c3[i, k] = combine([c2[i, j] for j in range(NZ)])
        for j, f, where in peers():
            send(c3.at[i, k], c3.at[i, k], s3.at[i, j], r3.at[i, k], where)
        MX[...] = jnp.zeros((ROWS, 128), F32)
        use(k, c3[i, k])
        for j, f, where in list(peers())[::-1]:
            landed(c3.at[i, f], s3.at[i, j], r3.at[i, f], where)
            use(f, c3[i, f])
        return row_form(MX[...])

    def group(f):
        return pl.ds(pl.multiple_of(f * GROUP, GROUP), GROUP)

    def row_add(f, keep):
        def block(b, _):
            at = pl.ds(pl.multiple_of(b * 64, 64), 64)
            acc = [MX[at, :], jnp.zeros((64, 128), F32)]
            for j in range(GROUP):
                t = f * GROUP + j
                term = S[t, at, :] * W[pl.ds(t, 1), :]
                if keep:
                    S[t, at, :] = term
                acc[j % 2] = acc[j % 2] + term
            MX[at, :] = acc[0] + acc[1]
            return 0
        lax.fori_loop(0, 4, block, 0)

    def col_piece(weights, f):
        def tile(q, _):
            t = f * GROUP + 4 * q
            acc = [None] * 4
            for b in range(4):
                at = slice(b * 64, (b + 1) * 64)
                w = weights[at, :]
                for j in range(4):
                    term = S[t + j, at, :] * w
                    acc[j] = term if b == 0 else acc[j] + term
            for j in range(4):
                CS[pl.ds(t + j, 1), :] = jnp.sum(acc[j], axis=0, keepdims=True)
            return 0
        lax.fori_loop(0, GROUP // 4, tile, 0)
        return CS[group(f), :]

    def bulk_one():
        pass

    f_one = -LOG2_B - row_all(0, loc, lse2, bulk_one)
    FB[...] = spread(f_one)
    FG[x, z, 0:1] = f_one[:, :128]
    FG[x, z, 1:2] = f_one[:, 128:]
    for d in range(1, NZ):
        send(FG.at[x, z], FG.at[x, z], fs.at[0, d], fr.at[0, z], {"z": at_z(d)})

    def tops(t):
        best = [None, None]
        for b in range(4):
            at = slice(b * 64, (b + 1) * 64)
            f = FB[at, :]
            for j in range(2):
                here = S[t + j, at, :] + f
                best[j] = here if b == 0 else jnp.maximum(best[j], here)
        return tuple(jnp.max(m, axis=0, keepdims=True) for m in best)

    def plan_piece(f):
        start = f * GROUP

        def tile(q, m):
            t = start + 2 * q
            later = tops(jnp.minimum(t + 2, start + GROUP - 2))
            acc = [None, None]
            for b in range(4):
                at = slice(b * 64, (b + 1) * 64)
                fb = FB[at, :]
                for j in range(2):
                    e = jnp.exp2(S[t + j, at, :] + fb - m[j])
                    S[t + j, at, :] = e
                    acc[j] = e if b == 0 else acc[j] + e
            for j in range(2):
                CM[pl.ds(t + j, 1), :] = m[j]
                CS[pl.ds(t + j, 1), :] = jnp.sum(acc[j], axis=0, keepdims=True)
            return later

        lax.fori_loop(0, GROUP // 2, tile, tops(start))
        at = group(f)
        return CM[at, :] + jnp.log(CS[at, :]) * LOG2E

    chip = x * NZ + z
    pown = PV.at[pl.ds(pl.multiple_of(chip * 512, 512), 512)]

    def own_cols(ref, out):
        for j in range(4):
            out[j * 128:(j + 1) * 128, :] = spread(ref[pl.ds(chip * 4 + j, 1), :])

    def back_plan(n, theirs):
        zb = at_z(offset(n, 1 - parity if theirs else parity))
        if theirs:
            if n == 0:
                @pl.when(parity == 0)
                def _():
                    y_first(zb).wait_recv()

            for d in range(1 if n == 0 else 0, NX):
                f = at_x(d)
                landed(EA.at[f, zb], es_y.at[n, d], er.at[f, zb], {"p": at_y(-1 if d < 2 else 1)})

        def block(xb, _):
            s = dot_nt(pown[...], EA[xb, zb]) * SCALE2
            for i in range(2):
                NP[xb * NZ + zb, :, i * 128:(i + 1) * 128] = jnp.exp2(
                    (s[:, i * 128:(i + 1) * 128] - LB[...]) + FG[xb, zb, i:i + 1])
            return 0

        lax.fori_loop(0, NX, block, 0)

    def share_f():
        x_stage(1)
        y_stage(0)
        for d in range(1, NZ):
            f = at_z(d)
            landed(FG.at[x, f], fs.at[0, d], fr.at[0, f], {"z": f})
        for d in range(1, NX):
            send(FG.at[x], FG.at[x], fs.at[1, d], fr.at[1, x], {"x": at_x(d)})

    def use_one(f, big):
        at = group(f)
        LG[at, :] = big
        D[at, :] = jnp.exp2(big) * N_B
        W[at, :] = jnp.exp2(CM[at, :] - big)
        row_add(f, True)

    def fill_row_two():
        x_stage(2)
        own_cols(LG, LB)
        for d in range(1, NX):
            f = at_x(d)
            landed(FG.at[f], fs.at[1, d], fr.at[1, f], {"x": f})
        back_plan(0, False)

    mass = col_round(0, plan_piece, lse2, share_f, lambda: None, use_one)
    u = (N_K / N_B) / row_all(1, mass, total, fill_row_two)
    UB[...] = spread(u)

    def use_two(f, col):
        at = group(f)
        V[at, :] = ccot_ref[at, :] * (-1.0 / col)
        W[at, :] = V[at, :]
        row_add(f, False)

    def fill_col_two():
        y_stage(2)
        back_plan(0, True)

    def fill_row_three():
        own_cols(V, AB)
        back_plan(2, False)

    def fill_col_two_first():
        x_stage(3)
        y_stage(1)
        back_plan(1, False)

    moved = col_round(1, lambda f: col_piece(UB, f), total, fill_col_two_first, fill_col_two, use_two)
    bar_two = rcot_ref[...] + u * row_all(2, moved, total, fill_row_three)
    xr = bar_two * u
    XB[...] = spread(xr)
    xn = xr * -(N_B / N_K)
    for j, vec in enumerate((u, xn)):
        G[x, z, 2 * j:2 * j + 1] = vec[:, :128]
        G[x, z, 2 * j + 1:2 * j + 2] = vec[:, 128:]
    for d in range(1, NZ):
        send(G.at[x, z], G.at[x, z], gs.at[0, d], gr.at[x, z], {"z": at_z(d)})

    def use_three(f, col):
        at = group(f)
        NB[at, :] = col * (N_B / N_K)
        W[at, :] = NB[at, :]
        row_add(f, False)

    def fill_col_three():
        for d in range(1, NZ):
            f = at_z(d)
            landed(G.at[x, f], gs.at[0, d], gr.at[x, f], {"z": f})
        for d in range(1, NX):
            send(G.at[x], G.at[x], gs.at[1, d], yr.at[0, x], {"x": at_x(d)})
        back_plan(3, False)
        back_plan(2, True)

    def fill_row_four():
        XB[...] = XB[...] * -(N_B / N_K)
        own_cols(NB, CB)
        own_cols(D, DB)
        back_plan(3, True)

    def fill_col_three_first():
        y_stage(3)
        back_plan(1, True)

    last = col_round(2, lambda f: col_piece(XB, f), total, fill_col_three_first, fill_col_three, use_three)
    yn = -row_all(3, last, total, fill_row_four)
    Y[x, z, 0:1] = yn[:, :128]
    Y[x, z, 1:2] = yn[:, 128:]
    for d in range(1, NZ):
        send(Y.at[x, z], Y.at[x, z], ys.at[0, d], gr.at[NX + x, z], {"z": at_z(d)})
    FB[...] = spread(yn)
    RP[...] = jnp.zeros((ROWS, WIDTH), F32)

    HALF = ROWS // 2
    piece = ROWS // NY

    def adjoint_rows(q, n, h):
        for b in range(4):
            at = slice(h * HALF + b * 32, h * HALF + (b + 1) * 32)
            ub, xb, yb = UB[at, :], XB[at, :], FB[at, :]
            for j in range(8):
                t = 8 * q + j
                g = (ub * V[pl.ds(t, 1), :] + xb) + (yb * D[pl.ds(t, 1), :] + NB[pl.ds(t, 1), :])
                ADJ[n, b * 32:(b + 1) * 32, j * 128:(j + 1) * 128] = (S[t, at, :] * g).astype(BF16)

    def row_grad(q, n, h):
        at = pl.multiple_of(q * 1024, 1024)
        rows = slice(h * HALF, (h + 1) * HALF)
        RP[rows, :] += jnp.dot(ADJ[n], PV[pl.ds(at, 1024), :], preferred_element_type=F32)

    def grad_half(h):
        def grad_chunk(q, _):
            row_grad(2 * q - 1, 1, h)
            adjoint_rows(2 * q, 0, h)
            row_grad(2 * q, 0, h)
            adjoint_rows(2 * q + 1, 1, h)
            return 0

        adjoint_rows(0, 0, h)
        row_grad(0, 0, h)
        adjoint_rows(1, 1, h)
        lax.fori_loop(1, COLS // 2048, grad_chunk, 0)
        row_grad(COLS // 1024 - 1, 1, h)
        for j in range(2 * h, 2 * h + 2):
            EB[j, y] = RP[j * piece:(j + 1) * piece, :]

            @pl.when(y != j)
            def _():
                eb_copy(j).start()

    def eb_copy(j):
        return pltpu.make_async_remote_copy(
            src_ref=EB.at[j, y], dst_ref=EB.at[j, y], send_sem=eb_s.at[j], recv_sem=eb_r.at[y],
            device_id={"p": j}, device_id_type=MESH)

    grad_half(0)
    for d in range(1, NZ):
        f = at_z(d)
        landed(Y.at[x, f], ys.at[0, d], gr.at[NX + x, f], {"z": f})
    for d in range(1, NX):
        send(Y.at[x], Y.at[x], ys.at[1, d], yr.at[1, x], {"x": at_x(d)})
    grad_half(1)

    PG[...] = jnp.zeros((2 * ROWS, WIDTH), F32)
    for d in range(1, NX):
        f = at_x(d)
        landed(G.at[f], gs.at[1, d], yr.at[0, f], {"x": f})
        landed(Y.at[f], ys.at[1, d], yr.at[1, f], {"x": f})

    def back_adjoint(o, n, m):
        xb, zb = o // NZ, o % NZ
        for b in range(16):
            at = slice(b * 32, (b + 1) * 32)
            a, g0, d = AB[at, :], CB[at, :], DB[at, :]
            for i in range(2):
                g = (a * G[xb, zb, i:i + 1] + G[xb, zb, 2 + i:3 + i]) + (g0 + d * Y[xb, zb, i:i + 1])
                to = slice(n * 256 + i * 128, n * 256 + (i + 1) * 128)
                ADJ2[m, at, to] = (NP[o, at, i * 128:(i + 1) * 128] * g).astype(BF16)

    def back_grad(o, m):
        rows = EA[o // NZ, pl.ds(o % NZ, 2)].reshape(2 * ROWS, WIDTH)
        PG[...] += jnp.dot(ADJ2[m], rows, preferred_element_type=F32)

    def back_block(q, _):
        o = 4 * q
        back_grad(o - 2, 1)
        back_adjoint(o, 0, 0)
        back_adjoint(o + 1, 1, 0)
        back_grad(o, 0)
        back_adjoint(o + 2, 0, 1)
        back_adjoint(o + 3, 1, 1)
        return 0

    def share_rows():
        for d in range(1, NY):
            f = at_y(d)
            landed(EB.at[y, f], eb_s.at[0], eb_r.at[f], {"p": f})
        EO[y] = total([EB[y, j] for j in range(NY)]) * SCALE
        for d in range(1, NY):
            send(EO.at[y], EO.at[y], eo_s.at[d], eo_r.at[y], {"p": at_y(d)})

    back_adjoint(0, 0, 0)
    back_adjoint(1, 1, 0)
    back_grad(0, 0)
    back_adjoint(2, 0, 1)
    back_adjoint(3, 1, 1)
    lax.fori_loop(1, 4, back_block, 0)
    share_rows()
    lax.fori_loop(4, NX * NZ // 4, back_block, 0)
    back_grad(NX * NZ - 2, 1)
    there = PG.at[pl.ds(pl.multiple_of((1 - c) * ROWS, ROWS), ROWS)]
    send(there, PR, pr_s, pr_r, {"c": 1 - c})
    for d in range(1, NY):
        f = at_y(d)
        landed(EO.at[f], eo_s.at[d], eo_r.at[f], {"p": f})
    eg_ref[...] = EO[...].reshape(ROWS, WIDTH)
    landed(PR, pr_s, pr_r, {"c": 1 - c})
    pg_ref[...] = (PG[pl.ds(pl.multiple_of(c * ROWS, ROWS), ROWS), :] + PR[...]) * SCALE
    @pl.when(parity == 1)
    def _():
        y_first(z).wait_send()

    for n in range(4):
        z_sent(n)

        @pl.when(y != n)
        def _():
            eb_copy(n).wait_send()
    for copy in sent:
        copy.wait_send()


def step(embeddings, prototypes, row_cot, col_cot):
    vm = pltpu.VMEM
    dma = pltpu.SemaphoreType.DMA
    wide = vm((ROWS, 128), F32)
    line = vm((TILES, 128), F32)
    scratch = [
        vm((TILES, ROWS, 128), F32), vm((COLS, WIDTH), BF16), vm((NX, NZ, ROWS, WIDTH), BF16),
        wide, wide, wide, wide,
        line, line, line, line, line, line, line,
        vm((2, ROWS // 2, 1024), BF16), vm((ROWS, WIDTH), F32), vm((2 * ROWS, WIDTH), F32), vm((ROWS, WIDTH), F32),
        vm((512, 128), F32), vm((512, 128), F32), vm((512, 128), F32), vm((512, 128), F32), vm((2, 512, 512), BF16), vm((NX * NZ, 512, ROWS), F32), vm((2, ROWS, 512), F32),
        vm((4, NY, 1, ROWS), F32), vm((3, 8, TILES // 8, 128), F32), vm((3, 8, TILES // 8, 128), F32),
        vm((3, NZ, TILES // 8, 128), F32), vm((3, 8, TILES // 8, 128), F32),
        vm((NX, NZ, 4, 128), F32), vm((NX, NZ, 2, 128), F32), vm((NX, NZ, 2, 128), F32),
        vm((NY, NY, ROWS // NY, WIDTH), F32), vm((NY, ROWS // NY, WIDTH), F32),
        dma((8,)), dma(()), dma((4, NY)), dma((4, NY)),
        dma((3, 8)), dma((3, 8)), dma((3, 8)), dma((3, 8)), dma((3, 8)), dma((3, 8)),
        dma((4,)), dma((4, NX)), dma((4, NX)), dma((NX, NZ)), dma((2, NZ)), dma((2 * NX, NZ)),
        dma((2, NZ)), dma((2, NX)), dma((2, NZ)), dma((2, NZ)),
        dma((NY,)), dma((NY,)), dma((NY,)), dma((NY,)), dma(()), dma(()),
    ]
    anywhere = pl.BlockSpec(memory_space=pl.ANY)
    inside = pl.BlockSpec(memory_space=pltpu.VMEM)
    return pl.pallas_call(
        kernel,
        out_shape=(jax.ShapeDtypeStruct((ROWS, WIDTH), F32), jax.ShapeDtypeStruct((ROWS, WIDTH), F32)),
        in_specs=[anywhere, anywhere, inside, inside],
        out_specs=(inside, inside),
        scratch_shapes=scratch,
        compiler_params=pltpu.CompilerParams(collective_id=0, has_side_effects=True, vmem_limit_bytes=60 << 20),
        name="sinkhorn_back",
    )(embeddings, prototypes, row_cot.reshape(1, ROWS), col_cot.reshape(TILES, 128))


def solution(mesh):
    split = Mesh(mesh.devices.reshape(NX, NZ, NC, NY), ("x", "z", "c", "p"))
    rows = ("x", "z", "c")
    return jax.shard_map(
        step,
        mesh=split,
        in_specs=(P(rows, None), P("p", None), P(rows), P("p")),
        out_specs=(P(rows, None), P(("p",) + rows, None)),
        check_vma=False,
    )
```
